32 devices in a mesh: row: 4 (over y, x), col: 8 (over z, core).
Axes of the slice: x: 2, y: 2, z: 4, core: 2. Of those that a mesh axis runs over, the one named last changes fastest.
Arguments:
- source: float32 [8192, 128], P(('row', 'col')), may hold values from -6 to 6
- value: bfloat16 [8192, 8192], P('row', 'col'), may hold values from -128 to 127, as said below
- occupancy: int32 [64, 64], P('row', 'col'), may hold values 0 or 1
- exponent: int32 [64, 64], P('row', 'col'), may hold values from -3 to 3, as said below
Outputs:
- diffused: float32 [8192, 128], P(('row', 'col'))
The draws below stay inside these ranges and needn't reach their ends.
Inputs may be any that keep to these rules, and one draw needn't show every extreme that they name: `value`: whole numbers, drawn independently; both ends of the range occur. `exponent`: tile exponents; every value of the range occurs.
All inputs are finite; a program needn't handle non-finite values. No bound on the sum of `occupancy` on one device may be relied on, other than what follows from the above.
Results may differ from the reference program's by a relative error of at most 0.0003.
Values sent between devices are 32-bit elements; how exact they have to be, the bound alone decides.
No kernel may reach another device: no remote copies, remote signals or barrier semaphores. Data moves between devices by JAX's collectives and lax.ppermute only.
A program may use at most 128 MiB of HBM per device.

```python
import jax
import jax.numpy as jnp
from jax import lax

FEATURES = 128
SPAN = 256
STEPS = 3
BLOCK = 128
NODES = 8192
N_ROW = 4
N_COL = 8


def draw_value(key, part):
    entry_key, pick_key = jax.random.split(jax.random.fold_in(key, 29))
    row_pick, high_col, low_col = jax.random.split(pick_key, 3)
    entries = jax.random.randint(entry_key, (NODES, NODES), -128, 128, dtype=jnp.int32)
    top_row = jax.random.randint(row_pick, (), 0, NODES, dtype=jnp.int32)
    bottom_row = (top_row + 1) % NODES
    top_col = jax.random.randint(high_col, (), 0, NODES, dtype=jnp.int32)
    bottom_col = jax.random.randint(low_col, (), 0, NODES, dtype=jnp.int32)
    row_index = jnp.arange(NODES, dtype=jnp.int32)[:, None]
    col_index = jnp.arange(NODES, dtype=jnp.int32)[None, :]
    entries = jnp.where((row_index == top_row) & (col_index == top_col), jnp.int32(127), entries)
    entries = jnp.where((row_index == bottom_row) & (col_index == bottom_col), jnp.int32(-128), entries)
    return entries.astype(jnp.float32).astype(jnp.bfloat16)


def draw_exponent(key, part):
    nblocks = NODES // BLOCK
    first_key, second_key = jax.random.split(jax.random.fold_in(key, 17))
    row_level = (jax.random.permutation(first_key, nblocks) % 4).astype(jnp.int32)
    offset = jax.random.randint(second_key, (), 0, 2, dtype=jnp.int32)
    columns = jnp.arange(nblocks, dtype=jnp.int32)
    col_level = (columns + offset) % 2
    rising = 3 * columns // nblocks
    return (row_level[:, None] + col_level[None, :] + rising[None, :] - 3).astype(jnp.int32)


def plant(values, key, least, top_value):
    extent = values.shape
    place = [jax.random.randint(jax.random.fold_in(key, axis), (), 0, extent[axis]) for axis in range(len(extent))]
    values = values.at[tuple(place)].set(least)
    longest = extent.index(max(extent))
    place[longest] = (place[longest] + 1) % extent[longest]
    return values.at[tuple(place)].set(top_value)


def level_of(key, dims, cuts, smallest, top_value):
    gain, own = 1.0, jax.random.fold_in(key, 6)
    for position, parts in cuts:
        draws = jnp.exp(jax.random.uniform(jax.random.fold_in(own, position), (parts,), jnp.float32, smallest / len(cuts), top_value / len(cuts)))
        gain = gain * jnp.repeat(draws, dims[position] // parts).reshape([-1 if axis == position else 1 for axis in range(len(dims))])
    return gain


def noise(own_key, dims, deviation, limit, cuts=(), kind=jnp.bfloat16):
    array = deviation * jax.random.normal(own_key, dims, jnp.float32)
    if cuts:
        array = array * level_of(own_key, dims, cuts, -0.22, 0.18)
    return jnp.clip(array, -limit, limit).astype(kind)


def setup_inputs(seed: int = 0) -> dict:
    arg_keys = jax.random.split(jax.random.key(seed), 5)
    source = noise(arg_keys[0], (NODES, FEATURES), 1.0, 6.0, ((0, 32),), jnp.float32)
    value = draw_value(jax.random.fold_in(arg_keys[4], 71), 0)
    occupancy = plant((jax.random.randint(arg_keys[2], (NODES // BLOCK, NODES // BLOCK), 0, 2) < 1).astype(jnp.int32), jax.random.fold_in(arg_keys[2], 1), 0, 1)
    exponent = draw_exponent(jax.random.fold_in(arg_keys[4], 71), 0)
    return {"source": source, "value": value, "occupancy": occupancy, "exponent": exponent}


EPSILON = 1e-05
RETAIN = 0.8
TELEPORT = 0.2

def block_values(value_rows, occupied_rows, exponent_rows):
    row_count = value_rows.shape[0]
    dense_tile = value_rows.astype(jnp.float32)
    scales = occupied_rows.astype(jnp.float32) * jnp.exp2(exponent_rows.astype(jnp.float32))
    blocked = dense_tile.reshape(row_count // BLOCK, BLOCK, NODES // BLOCK, BLOCK) * scales[:, None, :, None]
    return blocked.reshape(row_count, NODES)

def reference(source, value, occupancy, exponent):
    row_count = NODES // N_ROW

    def propagate(current):
        permuted = current.reshape(N_ROW, N_COL, SPAN, FEATURES).transpose(1, 0, 2, 3).reshape(NODES, FEATURES)

        def row_group(group_index):
            first_row = group_index * row_count
            first_block = group_index * (row_count // BLOCK)
            value_rows = lax.dynamic_slice_in_dim(value, first_row, row_count, 0)
            occupied_rows = lax.dynamic_slice_in_dim(occupancy, first_block, row_count // BLOCK, 0)
            exponent_rows = lax.dynamic_slice_in_dim(exponent, first_block, row_count // BLOCK, 0)
            dense_tile = block_values(value_rows, occupied_rows, exponent_rows)
            energy = lax.optimization_barrier(jnp.sum(dense_tile * dense_tile, axis=1))
            inverse = 1.0 / (jnp.sqrt(NODES * 1.0) * jnp.sqrt(energy / NODES + EPSILON))
            product = jnp.dot(dense_tile, permuted, precision=lax.Precision.HIGHEST, preferred_element_type=jnp.float32)
            return product * inverse[:, None]
        mixing = lax.map(row_group, jnp.arange(N_ROW, dtype=jnp.int32))
        return mixing.reshape(NODES, FEATURES)
    current = source
    for iteration in range(STEPS):
        current = jnp.tanh(RETAIN * propagate(current) + TELEPORT * source)
    return current
```

```python
import functools

import jax
import jax.numpy as jnp
from jax import lax
from jax.experimental import pallas as pl
from jax.experimental.pallas import tpu as pltpu
from jax.sharding import PartitionSpec as P

STEPS = 3
TILE = 128
EPSILON = 1e-05
RETAIN = 0.8
TELEPORT = 0.2
VMEM = pl.BlockSpec(memory_space=pltpu.VMEM)


def params(mib):
    return pltpu.CompilerParams(vmem_limit_bytes=mib * 1024 * 1024)


def swap(array, axis, size, offset):
    return lax.ppermute(array, axis, [(i, i ^ offset) for i in range(size)])


def prepare_kernel(chunks, span, rows_ref, cols_ref, scale_ref, value_ref, out_ref, energy_ref):
    block = rows_ref[pl.program_id(0)]
    parts = span // TILE
    for half in range(parts):
        rows = slice(half * TILE, (half + 1) * TILE)
        total = jnp.zeros((TILE, TILE), jnp.float32)
        for chunk in range(chunks):
            for part in range(parts):
                tile = cols_ref[chunk] * parts + part
                scale = scale_ref[block * parts + half, tile]
                source = pl.ds(pl.multiple_of(tile * TILE, TILE), TILE)
                scaled = value_ref[rows, source].astype(jnp.float32) * scale
                total += scaled * scaled
                target = chunk * span + part * TILE
                out_ref[rows, target : target + TILE] = scaled.astype(jnp.bfloat16)
        energy_ref[0, :, rows] = lax.dot_general(
            jnp.ones((8, TILE), jnp.float32),
            total,
            (((1,), (1,)), ((), ())),
            precision=lax.Precision.HIGHEST,
            preferred_element_type=jnp.float32,
        )


def prepare(value, scales, row_order, col_order, span):
    row_count, col_count = value.shape
    blocks = row_count // span
    return pl.pallas_call(
        functools.partial(prepare_kernel, col_count // span, span),
        grid_spec=pltpu.PrefetchScalarGridSpec(
            num_scalar_prefetch=3,
            grid=(blocks,),
            in_specs=[pl.BlockSpec((span, col_count), lambda i, rows, cols, scale: (rows[i], 0))],
            out_specs=[
                pl.BlockSpec((span, col_count), lambda i, rows, cols, scale: (i, 0)),
                pl.BlockSpec((1, 8, span), lambda i, rows, cols, scale: (i, 0, 0)),
            ],
        ),
        out_shape=[
            jax.ShapeDtypeStruct(value.shape, jnp.bfloat16),
            jax.ShapeDtypeStruct((blocks, 8, span), jnp.float32),
        ],
        compiler_params=params(12),
        name="prepare",
    )(row_order, col_order, scales, value)


def inverse_kernel(nodes, energy_ref, out_ref):
    energy = lax.dot_general(
        energy_ref[...],
        jnp.full((8, TILE), 0.125, jnp.float32),
        (((0,), (0,)), ((), ())),
        precision=lax.Precision.HIGHEST,
        preferred_element_type=jnp.float32,
    )
    norm = jnp.sqrt(jnp.float32(nodes)) * jnp.sqrt(energy / nodes + EPSILON)
    out_ref[...] = 1.0 / norm


def inverse_of(energy, nodes):
    return pl.pallas_call(
        functools.partial(inverse_kernel, nodes),
        out_shape=jax.ShapeDtypeStruct((energy.shape[1], TILE), jnp.float32),
        in_specs=[VMEM],
        out_specs=VMEM,
        compiler_params=params(4),
        name="inverse",
    )(energy)


def multiply_kernel(first_row, first, count, add, adjacency_ref, *refs):
    features, refs = refs[:count], refs[count:]
    total_ref = refs[0] if add else None
    out_ref, both_ref = refs[-2:]
    span, width = features[0].shape
    for i in range(count):
        x = features[i][...]
        high = x.astype(jnp.bfloat16)
        rows = slice(i * span, (i + 1) * span)
        both_ref[rows, :width] = high
        both_ref[rows, width:] = (x - high.astype(jnp.float32)).astype(jnp.bfloat16)
    tile = 256

    def body(i, carry):
        here = pl.ds(pl.multiple_of(i * tile, tile), tile)
        rows = pl.ds(pl.multiple_of(first_row + i * tile, tile), tile)
        both = jnp.dot(
            adjacency_ref[rows, first * span : (first + count) * span],
            both_ref[...],
            preferred_element_type=jnp.float32,
        )
        sums = both[:, :width] + both[:, width:]
        if add:
            sums += total_ref[rows, :]
        out_ref[here, :] = sums
        return carry

    lax.fori_loop(0, out_ref.shape[0] // tile, body, 0)


def multiply(adjacency, first_row, row_count, first, features, total=None):
    span, width = features[0].shape
    count = len(features)
    add = total is not None
    return pl.pallas_call(
        functools.partial(multiply_kernel, first_row, first, count, add),
        out_shape=jax.ShapeDtypeStruct((row_count, width), jnp.float32),
        in_specs=[VMEM] * (1 + count + add),
        out_specs=VMEM,
        scratch_shapes=[pltpu.VMEM((count * span, 2 * width), jnp.bfloat16)],
        compiler_params=params(4),
        cost_estimate=pl.CostEstimate(
            flops=4 * row_count * count * span * width,
            bytes_accessed=2 * row_count * count * span,
            transcendentals=0,
        ),
        name="multiply",
    )(adjacency, *features, *([total] if add else []))


def shards(source, value, occupancy, exponent):
    row_size, col_size = lax.axis_size("row"), lax.axis_size("col")
    span = source.shape[0]
    nodes = value.shape[0] * row_size
    row, col = lax.axis_index("row"), lax.axis_index("col")
    groups = col_size // 2
    offsets = jnp.arange(groups, dtype=jnp.int32) * 2
    row_order = jnp.concatenate([(col ^ 1) ^ offsets, col ^ offsets])
    col_order = row ^ jnp.arange(row_size, dtype=jnp.int32)
    scales = occupancy.astype(jnp.float32) * jnp.exp2(exponent.astype(jnp.float32))
    adjacency, energy = prepare(value, scales, row_order, col_order, span)
    half = groups * span

    def gather(current):
        return [current] + [swap(current, "row", row_size, d) for d in range(1, row_size)]

    pair = swap(energy[:groups], "col", col_size, 1) + energy[groups:]
    total = pair[0]
    for d in range(1, groups):
        total += swap(pair[d], "col", col_size, 2 * d)
    inverse = inverse_of(total, nodes)

    current = source
    for step in range(STEPS):
        features = gather(current)
        first = multiply(adjacency, 0, 2 * half, 0, features[:1])
        if row_size > 2:
            first = multiply(adjacency, 0, 2 * half, 1, features[1:-1], first)
        last = features[-1:]
        other = multiply(adjacency, 0, half, row_size - 1, last, first)
        moved = swap(other, "col", col_size, 1)
        mine = multiply(adjacency, half, half, row_size - 1, last, first)
        sums = [
            mine[d * span : (d + 1) * span] + moved[d * span : (d + 1) * span] for d in range(groups)
        ]
        product = sums[0]
        for d in range(1, groups):
            product += swap(sums[d], "col", col_size, 2 * d)
        current = jnp.tanh(RETAIN * (product * inverse) + TELEPORT * source)
    return current


def solution(mesh):
    placed = (P(("row", "col"), None), P("row", "col"), P("row", "col"), P("row", "col"))
    return jax.shard_map(
        shards, mesh=mesh, in_specs=placed, out_specs=P(("row", "col"), None), check_vma=False
    )
```

```python
import functools

import jax
import jax.numpy as jnp
from jax import lax
from jax.experimental import pallas as pl
from jax.experimental.pallas import tpu as pltpu
from jax.sharding import PartitionSpec as P


STEPS = 3
TILE = 128
EPSILON = 1e-05
RETAIN = 0.8
TELEPORT = 0.2
VMEM = pl.BlockSpec(memory_space=pltpu.VMEM)


def params(mib):
    return pltpu.CompilerParams(vmem_limit_bytes=mib * 1024 * 1024)


def swap(array, axis, size, offset):
    return lax.ppermute(array, axis, [(i, i ^ offset) for i in range(size)])


def prepare_kernel(chunks, rows_ref, cols_ref, present_ref, power_ref, value_ref, out_ref, energy_ref, held, arrived):
    blocks, span, _ = held.shape
    parts = span // TILE

    def copy(i):
        start = pl.multiple_of(rows_ref[i] * span, span)
        return pltpu.make_async_copy(value_ref.at[pl.ds(start, span)], held.at[i], arrived.at[i])

    for i in range(blocks):
        copy(i).start()

    def body(i, carry):
        copy(i).wait()
        for half in range(parts):
            rows = slice(half * TILE, (half + 1) * TILE)
            target_rows = pl.ds(pl.multiple_of(i * span + half * TILE, TILE), TILE)
            row_tile = rows_ref[i] * parts + half
            total = jnp.zeros((TILE, TILE), jnp.float32)
            for chunk in range(chunks):
                for part in range(parts):
                    tile = cols_ref[chunk] * parts + part
                    power = jnp.int32(1) << (power_ref[tile, row_tile] + 3)
                    scale = (present_ref[tile, row_tile] * power).astype(jnp.float32) * 0.125
                    from_cols = pl.ds(pl.multiple_of(tile * TILE, TILE), TILE)
                    scaled = held[i, rows, from_cols].astype(jnp.float32) * scale
                    total += scaled * scaled
                    target = chunk * span + part * TILE
                    out_ref[target_rows, target : target + TILE] = scaled.astype(jnp.bfloat16)
            energy_ref[target_rows, :] = total
        return carry

    lax.fori_loop(0, blocks, body, 0)


def prepare(value, present, power, row_order, col_order, span):
    row_count, col_count = value.shape
    blocks = row_count // span
    smem = pl.BlockSpec(memory_space=pltpu.SMEM)
    return pl.pallas_call(
        functools.partial(prepare_kernel, col_count // span),
        in_specs=[smem] * 4 + [pl.BlockSpec(memory_space=pltpu.HBM)],
        out_specs=[VMEM, VMEM],
        out_shape=[
            jax.ShapeDtypeStruct(value.shape, jnp.bfloat16),
            jax.ShapeDtypeStruct((row_count, TILE), jnp.float32),
        ],
        scratch_shapes=[
            pltpu.VMEM((blocks, span, col_count), jnp.bfloat16),
            pltpu.SemaphoreType.DMA((blocks,)),
        ],
        compiler_params=params(48),
        name="prepare",
    )(row_order, col_order, present.T, power.T, value)


def energy_kernel(total_ref, out_ref):
    total = total_ref[...]
    ones = jnp.ones((8, TILE), jnp.bfloat16)
    sums = jnp.zeros(out_ref.shape, jnp.float32)
    for _ in range(3):
        piece = total.astype(jnp.bfloat16)
        total -= piece.astype(jnp.float32)
        sums += lax.dot_general(
            ones, piece, (((1,), (1,)), ((), ())), preferred_element_type=jnp.float32
        )
    out_ref[...] = sums


def energy_of(total):
    return pl.pallas_call(
        energy_kernel,
        out_shape=jax.ShapeDtypeStruct((8, total.shape[0]), jnp.float32),
        in_specs=[VMEM],
        out_specs=VMEM,
        compiler_params=params(8),
        name="energy",
    )(total)


def inverse_kernel(nodes, energy_ref, out_ref):
    energy = lax.dot_general(
        energy_ref[...],
        jnp.full((8, TILE), 0.125, jnp.float32),
        (((0,), (0,)), ((), ())),
        precision=lax.Precision.HIGHEST,
        preferred_element_type=jnp.float32,
    )
    norm = jnp.sqrt(jnp.float32(nodes)) * jnp.sqrt(energy / nodes + EPSILON)
    out_ref[...] = 1.0 / norm


def inverse_of(energy, nodes):
    return pl.pallas_call(
        functools.partial(inverse_kernel, nodes),
        out_shape=jax.ShapeDtypeStruct((energy.shape[1], TILE), jnp.float32),
        in_specs=[VMEM],
        out_specs=VMEM,
        compiler_params=params(4),
        name="inverse",
    )(energy)


def multiply_kernel(first_row, first, count, add, adjacency_ref, *refs):
    features, refs = refs[:count], refs[count:]
    total_ref = refs[0] if add else None
    out_ref, both_ref = refs[-2:]
    span, width = features[0].shape
    for i in range(count):
        x = features[i][...]
        high = x.astype(jnp.bfloat16)
        rows = slice(i * span, (i + 1) * span)
        both_ref[rows, :width] = high
        both_ref[rows, width:] = (x - high.astype(jnp.float32)).astype(jnp.bfloat16)
    tile = min(out_ref.shape[0], 2048)
    for start in range(0, out_ref.shape[0], tile):
        rows = slice(first_row + start, first_row + start + tile)
        both = jnp.dot(
            adjacency_ref[rows, first * span : (first + count) * span],
            both_ref[...],
            preferred_element_type=jnp.float32,
        )
        sums = both[:, :width] + both[:, width:]
        if add:
            sums += total_ref[rows, :]
        out_ref[start : start + tile, :] = sums


def multiply(adjacency, first_row, row_count, first, features, total=None):
    span, width = features[0].shape
    count = len(features)
    add = total is not None
    return pl.pallas_call(
        functools.partial(multiply_kernel, first_row, first, count, add),
        out_shape=jax.ShapeDtypeStruct((row_count, width), jnp.float32),
        in_specs=[VMEM] * (1 + count + add),
        out_specs=VMEM,
        scratch_shapes=[pltpu.VMEM((count * span, 2 * width), jnp.bfloat16)],
        compiler_params=params(8),
        cost_estimate=pl.CostEstimate(
            flops=4 * row_count * count * span * width,
            bytes_accessed=2 * row_count * count * span,
            transcendentals=0,
        ),
        name="multiply",
    )(adjacency, *features, *([total] if add else []))


def shards(source, value, occupancy, exponent):
    row_size, col_size = lax.axis_size("row"), lax.axis_size("col")
    span = source.shape[0]
    nodes = value.shape[0] * row_size
    row, col = lax.axis_index("row"), lax.axis_index("col")
    groups = col_size // 2
    half = groups * span
    offsets = jnp.arange(groups, dtype=jnp.int32) * 2
    row_order = jnp.concatenate([(col ^ 1) ^ offsets, col ^ offsets])
    col_order = row ^ jnp.arange(row_size, dtype=jnp.int32)

    def owned(parts):
        total = parts[0]
        for d in range(1, groups):
            total += swap(parts[d], "col", col_size, 2 * d)
        return total

    current = source
    for step in range(STEPS):
        features = [current]
        for d in range(1, row_size):
            features.append(swap(current, "row", row_size, d))
        if step == 0:
            adjacency, squares = prepare(
                value, occupancy, exponent, row_order, col_order, span
            )
        first = multiply(adjacency, 0, 2 * half, 0, features[:1])
        if row_size > 2:
            first = multiply(adjacency, 0, 2 * half, 1, features[1:-1], first)
        last = features[-1:]
        other = multiply(adjacency, 0, half, row_size - 1, last, first)
        moved = swap(other, "col", col_size, 1)
        mine = multiply(adjacency, half, half, row_size - 1, last, first)
        product = owned(
            [
                mine[d * span : (d + 1) * span] + moved[d * span : (d + 1) * span]
                for d in range(groups)
            ],
        )
        if step == 0:
            energy = energy_of(squares)
            energy = energy[:, half:] + swap(energy[:, :half], "col", col_size, 1)
            energy = owned([energy[:, d * span : (d + 1) * span] for d in range(groups)])
            inverse = inverse_of(energy, nodes)
        current = jnp.tanh(RETAIN * (product * inverse) + TELEPORT * source)
    return current


def solution(mesh):
    placed = (P(("row", "col"), None), P("row", "col"), P("row", "col"), P("row", "col"))
    return jax.shard_map(
        shards, mesh=mesh, in_specs=placed, out_specs=P(("row", "col"), None), check_vma=False
    )
```

```python
import functools

import jax
import jax.numpy as jnp
from jax import lax
from jax.experimental import pallas as pl
from jax.experimental.pallas import tpu as pltpu
from jax.sharding import PartitionSpec as P


STEPS = 3
TILE = 128
EPSILON = 1e-05
RETAIN = 0.8
TELEPORT = 0.2
VMEM = pl.BlockSpec(memory_space=pltpu.VMEM)


def params(mib):
    return pltpu.CompilerParams(vmem_limit_bytes=mib * 1024 * 1024)


def swap(array, axis, size, offset):
    return lax.ppermute(array, axis, [(i, i ^ offset) for i in range(size)])


def prepare_kernel(chunks, rows_ref, cols_ref, scale_ref, value_ref, out_ref, energy_ref, held, arrived):
    blocks, span, _ = held.shape
    parts = span // TILE

    def copy(i):
        start = pl.multiple_of(rows_ref[i] * span, span)
        return pltpu.make_async_copy(value_ref.at[pl.ds(start, span)], held.at[i], arrived.at[i])

    for i in range(blocks):
        copy(i).start()

    def body(i, carry):
        copy(i).wait()
        for half in range(parts):
            from_rows = slice(half * TILE, (half + 1) * TILE)
            to_rows = pl.ds(pl.multiple_of(i * span + half * TILE, TILE), TILE)
            row_tile = rows_ref[i] * parts + half
            total = jnp.zeros((TILE, TILE), jnp.float32)
            for chunk in range(chunks):
                for part in range(parts):
                    tile = cols_ref[chunk] * parts + part
                    scale = scale_ref[tile, row_tile].astype(jnp.float32) * 0.125
                    from_cols = pl.ds(pl.multiple_of(tile * TILE, TILE), TILE)
                    scaled = held[i, from_rows, from_cols].astype(jnp.float32) * scale
                    total += scaled * scaled
                    target = chunk * span + part * TILE
                    out_ref[to_rows, target : target + TILE] = scaled.astype(jnp.bfloat16)
            energy_ref[to_rows, :] = total
        return carry

    lax.fori_loop(0, blocks, body, 0)


def prepare(value, present, power, row_order, col_order, span):
    row_count, col_count = value.shape
    blocks = row_count // span
    smem = pl.BlockSpec(memory_space=pltpu.SMEM)
    table = (present << (power + 3)).T
    return pl.pallas_call(
        functools.partial(prepare_kernel, col_count // span),
        in_specs=[smem] * 3 + [pl.BlockSpec(memory_space=pltpu.HBM)],
        out_specs=[VMEM, VMEM],
        out_shape=[
            jax.ShapeDtypeStruct(value.shape, jnp.bfloat16),
            jax.ShapeDtypeStruct((row_count, TILE), jnp.float32),
        ],
        scratch_shapes=[
            pltpu.VMEM((blocks, span, col_count), jnp.bfloat16),
            pltpu.SemaphoreType.DMA((blocks,)),
        ],
        compiler_params=params(48),
        name="prepare",
    )(row_order, col_order, table, value)


def energy_kernel(span, total_ref, out_ref):
    total = total_ref[...]
    ones = jnp.ones((8, TILE), jnp.bfloat16)
    sums = jnp.zeros((8, total.shape[0]), jnp.float32)
    for _ in range(3):
        piece = total.astype(jnp.bfloat16)
        total -= piece.astype(jnp.float32)
        sums += lax.dot_general(
            ones, piece, (((1,), (1,)), ((), ())), preferred_element_type=jnp.float32
        )
    out_ref[...] = jnp.zeros_like(out_ref)
    for block in range(sums.shape[1] // span):
        for part in range(span // TILE):
            start = block * span + part * TILE
            out_ref[block * 8 + part, :] = sums[0, start : start + TILE]


def energy_of(total, span):
    return pl.pallas_call(
        functools.partial(energy_kernel, span),
        out_shape=jax.ShapeDtypeStruct((total.shape[0] // span * 8, TILE), jnp.float32),
        in_specs=[VMEM],
        out_specs=VMEM,
        compiler_params=params(8),
        name="energy",
    )(total)


def combine_kernel(groups, mine_ref, moved_ref, energy_ref, energy_moved_ref, *out_refs):
    span = mine_ref.shape[0] // groups
    for d in range(groups):
        rows, small = slice(d * span, (d + 1) * span), slice(d * 8, (d + 1) * 8)
        mine = slice((groups + d) * 8, (groups + d + 1) * 8)
        out_refs[d][:span, :] = mine_ref[rows, :] + moved_ref[rows, :]
        out_refs[d][span:, :] = energy_ref[mine, :] + energy_moved_ref[small, :]


def combine(groups, mine, moved, energy, energy_moved):
    shape = (mine.shape[0] // groups + 8, mine.shape[1])
    return pl.pallas_call(
        functools.partial(combine_kernel, groups),
        out_shape=[jax.ShapeDtypeStruct(shape, jnp.float32)] * groups,
        in_specs=[VMEM] * 4,
        out_specs=[VMEM] * groups,
        compiler_params=params(4),
        name="combine",
    )(mine, moved, energy, energy_moved)


def finish_kernel(nodes, count, *refs):
    parts, (source_ref, current_ref, inverse_ref) = refs[:count], refs[count:]
    span = source_ref.shape[0]
    energy = parts[0][span:, :]
    product = parts[0][:span, :]
    for part in parts[1:]:
        energy += part[span:, :]
        product += part[:span, :]
    row = lax.broadcasted_iota(jnp.int32, (8, TILE), 0)
    for half in range(span // TILE):
        rows = slice(half * TILE, (half + 1) * TILE)
        column = lax.dot_general(
            energy,
            (row == half).astype(jnp.float32),
            (((0,), (0,)), ((), ())),
            precision=lax.Precision.HIGHEST,
            preferred_element_type=jnp.float32,
        )
        norm = jnp.sqrt(jnp.float32(nodes)) * jnp.sqrt(column / nodes + EPSILON)
        inverse = 1.0 / norm
        inverse_ref[rows, :] = inverse
        current_ref[rows, :] = jnp.tanh(
            RETAIN * (product[rows, :] * inverse) + TELEPORT * source_ref[rows, :]
        )


def finish(nodes, parts, source):
    shape = jax.ShapeDtypeStruct(source.shape, jnp.float32)
    return pl.pallas_call(
        functools.partial(finish_kernel, nodes, len(parts)),
        out_shape=[shape, shape],
        in_specs=[VMEM] * (len(parts) + 1),
        out_specs=[VMEM, VMEM],
        compiler_params=params(4),
        name="finish",
    )(*parts, source)


def fence_kernel(source_ref, out_ref):
    out_ref[...] = TELEPORT * source_ref[...]


def fence(source):
    return pl.pallas_call(
        fence_kernel,
        out_shape=jax.ShapeDtypeStruct(source.shape, jnp.float32),
        in_specs=[VMEM],
        out_specs=VMEM,
        compiler_params=params(4),
        cost_estimate=pl.CostEstimate(flops=10**10, bytes_accessed=10**8, transcendentals=0),
        name="fence",
    )(source)


def multiply_kernel(first_row, first, count, add, adjacency_ref, *refs):
    features, refs = refs[:count], refs[count:]
    total_ref = refs[0] if add else None
    out_ref, both_ref = refs[-2:]
    span, width = features[0].shape
    for i in range(count):
        x = features[i][...]
        high = x.astype(jnp.bfloat16)
        rows = slice(i * span, (i + 1) * span)
        both_ref[rows, :width] = high
        both_ref[rows, width:] = (x - high.astype(jnp.float32)).astype(jnp.bfloat16)
    tile = min(out_ref.shape[0], 2048)
    for start in range(0, out_ref.shape[0], tile):
        rows = slice(first_row + start, first_row + start + tile)
        both = jnp.dot(
            adjacency_ref[rows, first * span : (first + count) * span],
            both_ref[...],
            preferred_element_type=jnp.float32,
        )
        sums = both[:, :width] + both[:, width:]
        if add:
            sums += total_ref[rows, :]
        out_ref[start : start + tile, :] = sums


def multiply(adjacency, first_row, row_count, first, features, total=None):
    span, width = features[0].shape
    count = len(features)
    add = total is not None
    return pl.pallas_call(
        functools.partial(multiply_kernel, first_row, first, count, add),
        out_shape=jax.ShapeDtypeStruct((row_count, width), jnp.float32),
        in_specs=[VMEM] * (1 + count + add),
        out_specs=VMEM,
        scratch_shapes=[pltpu.VMEM((count * span, 2 * width), jnp.bfloat16)],
        compiler_params=params(8),
        cost_estimate=pl.CostEstimate(
            flops=4 * row_count * count * span * width,
            bytes_accessed=2 * row_count * count * span,
            transcendentals=0,
        ),
        name="multiply",
    )(adjacency, *features, *([total] if add else []))


def shards(source, value, occupancy, exponent):
    row_size, col_size = lax.axis_size("row"), lax.axis_size("col")
    span = source.shape[0]
    nodes = value.shape[0] * row_size
    row, col = lax.axis_index("row"), lax.axis_index("col")
    groups = col_size // 2
    half = groups * span
    offsets = jnp.arange(groups, dtype=jnp.int32) * 2
    row_order = jnp.concatenate([(col ^ 1) ^ offsets, col ^ offsets])
    col_order = row ^ jnp.arange(row_size, dtype=jnp.int32)

    def spread(parts):
        return [parts[0]] + [swap(parts[d], "col", col_size, 2 * d) for d in range(1, groups)]

    current = source
    for step in range(STEPS):
        features = [current]
        for d in range(1, row_size):
            features.append(swap(current, "row", row_size, d))
        if step == 0:
            teleport = fence(source)
            adjacency, squares = prepare(value, occupancy, exponent, row_order, col_order, span)
            energy = energy_of(squares, span)
            energy_moved = swap(energy[: 8 * groups], "col", col_size, 1)
        first = multiply(adjacency, 0, 2 * half, 0, features[:1])
        if row_size > 2:
            first = multiply(adjacency, 0, 2 * half, 1, features[1:-1], first)
        last = features[-1:]
        other = multiply(adjacency, 0, half, row_size - 1, last, first)
        moved = swap(other, "col", col_size, 1)
        mine = multiply(adjacency, half, half, row_size - 1, last, first)
        if step == 0:
            sums = combine(groups, mine, moved, energy, energy_moved)
            current, inverse = finish(nodes, spread(sums), source)
        else:
            sums = [
                mine[d * span : (d + 1) * span] + moved[d * span : (d + 1) * span]
                for d in range(groups)
            ]
            product = functools.reduce(jnp.add, spread(sums))
            current = jnp.tanh(RETAIN * (product * inverse) + teleport)
    return current


def solution(mesh):
    placed = (P(("row", "col"), None), P("row", "col"), P("row", "col"), P("row", "col"))
    return jax.shard_map(
        shards, mesh=mesh, in_specs=placed, out_specs=P(("row", "col"), None), check_vma=False
    )
```

```python
import functools

import jax
import jax.numpy as jnp
from jax import lax
from jax.experimental import pallas as pl
from jax.experimental.pallas import tpu as pltpu
from jax.sharding import PartitionSpec as P


STEPS = 3
TILE = 128
EPSILON = 1e-05
RETAIN = 0.8
TELEPORT = 0.2
VMEM = pl.BlockSpec(memory_space=pltpu.VMEM)


def params(mib):
    return pltpu.CompilerParams(vmem_limit_bytes=mib * 1024 * 1024)


def swap(array, axis, size, offset):
    return lax.ppermute(array, axis, [(i, i ^ offset) for i in range(size)])


def prepare_kernel(chunks, order_ref, scale_ref, value_ref, out_ref, energy_ref, held, arrived):
    blocks, span, _ = held.shape
    parts = span // TILE

    def copy(i):
        start = pl.multiple_of(order_ref[i] * span, span)
        return pltpu.make_async_copy(value_ref.at[pl.ds(start, span)], held.at[i], arrived.at[i])

    for i in range(blocks):
        copy(i).start()

    def body(i, carry):
        copy(i).wait()
        for half in range(parts):
            from_rows = slice(half * TILE, (half + 1) * TILE)
            to_rows = pl.ds(pl.multiple_of(i * span + half * TILE, TILE), TILE)
            row_tile = order_ref[i] * parts + half
            total = jnp.zeros((TILE, TILE), jnp.float32)
            for chunk in range(chunks):
                for part in range(parts):
                    tile = order_ref[blocks + chunk] * parts + part
                    scale = scale_ref[tile, row_tile].astype(jnp.float32) * 0.125
                    from_cols = pl.ds(pl.multiple_of(tile * TILE, TILE), TILE)
                    scaled = held[i, from_rows, from_cols].astype(jnp.float32) * scale
                    total += scaled * scaled
                    target = chunk * span + part * TILE
                    out_ref[to_rows, target : target + TILE] = scaled.astype(jnp.bfloat16)
            energy_ref[to_rows, :] = total
        return carry

    lax.fori_loop(0, blocks, body, 0)


def prepare(value, present, power, order, span):
    row_count, col_count = value.shape
    blocks = row_count // span
    smem = pl.BlockSpec(memory_space=pltpu.SMEM)
    table = (present << (power + 3)).T
    return pl.pallas_call(
        functools.partial(prepare_kernel, col_count // span),
        in_specs=[smem] * 2 + [pl.BlockSpec(memory_space=pltpu.HBM)],
        out_specs=[VMEM, VMEM],
        out_shape=[
            jax.ShapeDtypeStruct(value.shape, jnp.bfloat16),
            jax.ShapeDtypeStruct((row_count, TILE), jnp.float32),
        ],
        scratch_shapes=[
            pltpu.VMEM((blocks, span, col_count), jnp.bfloat16),
            pltpu.SemaphoreType.DMA((blocks,)),
        ],
        compiler_params=params(48),
        name="prepare",
    )(order, table, value)


def energy_kernel(span, total_ref, out_ref):
    total = total_ref[...]
    ones = jnp.ones((8, TILE), jnp.bfloat16)
    sums = jnp.zeros((8, total.shape[0]), jnp.float32)
    for _ in range(3):
        piece = total.astype(jnp.bfloat16)
        total -= piece.astype(jnp.float32)
        sums += lax.dot_general(
            ones, piece, (((1,), (1,)), ((), ())), preferred_element_type=jnp.float32
        )
    out_ref[...] = jnp.zeros_like(out_ref)
    for block in range(sums.shape[1] // span):
        for part in range(span // TILE):
            start = block * span + part * TILE
            out_ref[block * 8 + part, :] = sums[0, start : start + TILE]


def energy_of(total, span):
    return pl.pallas_call(
        functools.partial(energy_kernel, span),
        out_shape=jax.ShapeDtypeStruct((total.shape[0] // span * 8, TILE), jnp.float32),
        in_specs=[VMEM],
        out_specs=VMEM,
        compiler_params=params(8),
        name="energy",
    )(total)


def combine_kernel(first, groups, mine_ref, moved_ref, energy_ref, energy_moved_ref, *out_refs):
    count = len(out_refs)
    span = mine_ref.shape[0] // count
    for i in range(count):
        rows = slice(i * span, (i + 1) * span)
        theirs = slice((first + i) * 8, (first + i + 1) * 8)
        mine = slice((groups + first + i) * 8, (groups + first + i + 1) * 8)
        out_refs[i][:span, :] = mine_ref[rows, :] + moved_ref[rows, :]
        out_refs[i][span:, :] = energy_ref[mine, :] + energy_moved_ref[theirs, :]


def combine(first, count, groups, mine, moved, energy, energy_moved):
    shape = (mine.shape[0] // count + 8, mine.shape[1])
    return pl.pallas_call(
        functools.partial(combine_kernel, first, groups),
        out_shape=[jax.ShapeDtypeStruct(shape, jnp.float32)] * count,
        in_specs=[VMEM] * 4,
        out_specs=[VMEM] * count,
        compiler_params=params(4),
        name="combine",
    )(mine, moved, energy, energy_moved)


def finish_kernel(nodes, count, *refs):
    parts, (source_ref, current_ref, inverse_ref) = refs[:count], refs[count:]
    span = source_ref.shape[0]
    energy = parts[0][span:, :]
    product = parts[0][:span, :]
    for part in parts[1:]:
        energy += part[span:, :]
        product += part[:span, :]
    row = lax.broadcasted_iota(jnp.int32, (8, TILE), 0)
    for half in range(span // TILE):
        rows = slice(half * TILE, (half + 1) * TILE)
        column = lax.dot_general(
            energy,
            (row == half).astype(jnp.float32),
            (((0,), (0,)), ((), ())),
            precision=lax.Precision.HIGHEST,
            preferred_element_type=jnp.float32,
        )
        norm = jnp.sqrt(jnp.float32(nodes)) * jnp.sqrt(column / nodes + EPSILON)
        inverse = 1.0 / norm
        inverse_ref[rows, :] = inverse
        current_ref[rows, :] = jnp.tanh(
            RETAIN * (product[rows, :] * inverse) + TELEPORT * source_ref[rows, :]
        )


def finish(nodes, parts, source):
    shape = jax.ShapeDtypeStruct(source.shape, jnp.float32)
    return pl.pallas_call(
        functools.partial(finish_kernel, nodes, len(parts)),
        out_shape=[shape, shape],
        in_specs=[VMEM] * (len(parts) + 1),
        out_specs=[VMEM, VMEM],
        compiler_params=params(4),
        name="finish",
    )(*parts, source)


def order_kernel(offsets, chunks, out_ref):
    row, col = lax.axis_index("row"), lax.axis_index("col")
    blocks = 2 * len(offsets)
    for side in range(2):
        for i, offset in enumerate(offsets):
            out_ref[side * len(offsets) + i] = col ^ (2 * offset + 1 - side)
    for chunk in range(chunks):
        out_ref[blocks + chunk] = row ^ chunk


def order_of(offsets, chunks):
    return pl.pallas_call(
        functools.partial(order_kernel, offsets, chunks),
        out_shape=jax.ShapeDtypeStruct((2 * len(offsets) + chunks,), jnp.int32),
        out_specs=pl.BlockSpec(memory_space=pltpu.SMEM),
        compiler_params=params(1),
        cost_estimate=pl.CostEstimate(flops=10**10, bytes_accessed=10**8, transcendentals=0),
        name="order",
    )()


def multiply_kernel(first_row, first, count, add, adjacency_ref, *refs):
    features, refs = refs[:count], refs[count:]
    total_ref = refs[0] if add else None
    out_ref, both_ref = refs[-2:]
    span, width = features[0].shape
    for i in range(count):
        x = features[i][...]
        high = x.astype(jnp.bfloat16)
        rows = slice(i * span, (i + 1) * span)
        both_ref[rows, :width] = high
        both_ref[rows, width:] = (x - high.astype(jnp.float32)).astype(jnp.bfloat16)
    tile = min(out_ref.shape[0], 2048)
    for start in range(0, out_ref.shape[0], tile):
        rows = slice(first_row + start, first_row + start + tile)
        both = jnp.dot(
            adjacency_ref[rows, first * span : (first + count) * span],
            both_ref[...],
            preferred_element_type=jnp.float32,
        )
        sums = both[:, :width] + both[:, width:]
        if add:
            sums += total_ref[rows, :]
        out_ref[start : start + tile, :] = sums


def multiply(adjacency, first_row, row_count, first, features, total=None):
    span, width = features[0].shape
    count = len(features)
    add = total is not None
    return pl.pallas_call(
        functools.partial(multiply_kernel, first_row, first, count, add),
        out_shape=jax.ShapeDtypeStruct((row_count, width), jnp.float32),
        in_specs=[VMEM] * (1 + count + add),
        out_specs=VMEM,
        scratch_shapes=[pltpu.VMEM((count * span, 2 * width), jnp.bfloat16)],
        compiler_params=params(8),
        cost_estimate=pl.CostEstimate(
            flops=4 * row_count * count * span * width,
            bytes_accessed=2 * row_count * count * span,
            transcendentals=0,
        ),
        name="multiply",
    )(adjacency, *features, *([total] if add else []))


def far_offsets(groups):
    return [groups - 1] + list(range(1, groups - 1)) + [0] if groups > 1 else [0]


def shards(source, value, occupancy, exponent):
    row_size, col_size = lax.axis_size("row"), lax.axis_size("col")
    span = source.shape[0]
    nodes = value.shape[0] * row_size
    groups = col_size // 2
    half = groups * span
    offsets = far_offsets(groups)
    cuts = [(0, 1), (1, groups - 1)] if groups > 1 else [(0, 1)]

    order = order_of(offsets, row_size)
    current = source
    for step in range(STEPS):
        features = [current]
        for d in range(1, row_size):
            features.append(swap(current, "row", row_size, d))
        if step == 0:
            adjacency, squares = prepare(value, occupancy, exponent, order, span)
            energy = energy_of(squares, span)
            energy_moved = swap(energy[: 8 * groups], "col", col_size, 1)
        first = multiply(adjacency, 0, 2 * half, 0, features[:1])
        if row_size > 2:
            first = multiply(adjacency, 0, 2 * half, 1, features[1:-1], first)
        last = features[-1:]
        moved = []
        for start, count in cuts:
            other = multiply(adjacency, start * span, count * span, row_size - 1, last, first)
            moved.append(swap(other, "col", col_size, 1))
        sums = []
        for i, (start, count) in enumerate(cuts):
            mine = multiply(adjacency, half + start * span, count * span, row_size - 1, last, first)
            if step == 0:
                sums += combine(start, count, groups, mine, moved[i], energy, energy_moved)
            else:
                for d in range(count):
                    rows = slice(d * span, (d + 1) * span)
                    sums.append(mine[rows] + moved[i][rows])
        parts = [
            swap(part, "col", col_size, 2 * offset) if offset else part
            for offset, part in zip(offsets, sums)
        ]
        if step == 0:
            current, inverse = finish(nodes, parts, source)
        else:
            product = functools.reduce(jnp.add, parts)
            current = jnp.tanh(RETAIN * (product * inverse) + TELEPORT * source)
    return current


def solution(mesh):
    placed = (P(("row", "col"), None), P("row", "col"), P("row", "col"), P("row", "col"))
    return jax.shard_map(
        shards, mesh=mesh, in_specs=placed, out_specs=P(("row", "col"), None), check_vma=False
    )
```

```python
import functools

import jax
import jax.numpy as jnp
from jax import lax
from jax.experimental import pallas as pl
from jax.experimental.pallas import tpu as pltpu
from jax.sharding import PartitionSpec as P


STEPS = 3
TILE = 128
EPSILON = 1e-05
RETAIN = 0.8
TELEPORT = 0.2
VMEM = pl.BlockSpec(memory_space=pltpu.VMEM)


def params(mib):
    return pltpu.CompilerParams(vmem_limit_bytes=mib * 1024 * 1024)


def swap(array, axis, size, offset):
    return lax.ppermute(array, axis, [(i, i ^ offset) for i in range(size)])


def prepare_kernel(offsets, chunks, fence_ref, present_ref, power_ref, value_ref, out_ref, energy_ref, held, scales, arrived):
    blocks, span, _ = held.shape
    parts = span // TILE
    row, col = lax.axis_index("row"), lax.axis_index("col")
    sources = [col ^ (2 * offset + 1 - side) for side in range(2) for offset in offsets]

    def copy(i, chunk):
        rows = pl.ds(pl.multiple_of(sources[i] * span, span), span)
        cols = pl.ds(pl.multiple_of((row ^ chunk) * span, span), span)
        target = held.at[i, :, pl.ds(chunk * span, span)]
        return pltpu.make_async_copy(value_ref.at[rows, cols], target, arrived.at[i, chunk])

    for i in range(blocks):
        for chunk in range(chunks):
            copy(i, chunk).start()
    table = (present_ref[...] << (power_ref[...] + 3)).astype(jnp.float32) * 0.125
    shape = (table.shape[0], scales.shape[1])
    owner = lax.broadcasted_iota(jnp.int32, shape, 1) // TILE
    spread = owner == lax.broadcasted_iota(jnp.int32, shape, 0)
    scales[...] = lax.dot_general(
        table.astype(jnp.bfloat16),
        spread.astype(jnp.bfloat16),
        (((0,), (0,)), ((), ())),
        preferred_element_type=jnp.float32,
    )
    for i in range(blocks):
        for chunk in range(chunks):
            copy(i, chunk).wait()
        for half in range(parts):
            from_rows = slice(half * TILE, (half + 1) * TILE)
            to_rows = slice(i * span + half * TILE, i * span + (half + 1) * TILE)
            row_tile = pl.ds(sources[i] * parts + half, 1)
            total = jnp.zeros((TILE, TILE), jnp.float32)
            for chunk in range(chunks):
                cols = slice(chunk * span, (chunk + 1) * span)
                from_cols = pl.ds(pl.multiple_of((row ^ chunk) * span, span), span)
                scaled = held[i, from_rows, cols].astype(jnp.float32) * scales[row_tile, from_cols]
                out_ref[to_rows, cols] = scaled.astype(jnp.bfloat16)
                squares = scaled * scaled
                for part in range(parts):
                    total += squares[:, part * TILE : (part + 1) * TILE]
            energy_ref[to_rows, :] = total


def prepare(value, present, power, fence, offsets, span):
    row_count, col_count = value.shape
    blocks, chunks = row_count // span, col_count // span
    return pl.pallas_call(
        functools.partial(prepare_kernel, offsets, chunks),
        in_specs=[VMEM] * 3 + [pl.BlockSpec(memory_space=pltpu.HBM)],
        out_specs=[VMEM, VMEM],
        out_shape=[
            jax.ShapeDtypeStruct(value.shape, jnp.bfloat16),
            jax.ShapeDtypeStruct((row_count, TILE), jnp.float32),
        ],
        scratch_shapes=[
            pltpu.VMEM((blocks, span, col_count), jnp.bfloat16),
            pltpu.VMEM((row_count // TILE, col_count), jnp.float32),
            pltpu.SemaphoreType.DMA((blocks, chunks)),
        ],
        compiler_params=params(48),
        name="prepare",
    )(fence, present.T, power.T, value)


def energy_kernel(span, total_ref, out_ref):
    total = total_ref[...]
    ones = jnp.ones((8, TILE), jnp.bfloat16)
    sums = jnp.zeros((8, total.shape[0]), jnp.float32)
    for _ in range(3):
        piece = total.astype(jnp.bfloat16)
        total -= piece.astype(jnp.float32)
        sums += lax.dot_general(
            ones, piece, (((1,), (1,)), ((), ())), preferred_element_type=jnp.float32
        )
    out_ref[...] = jnp.zeros_like(out_ref)
    for block in range(sums.shape[1] // span):
        for part in range(span // TILE):
            start = block * span + part * TILE
            out_ref[block * 8 + part, :] = sums[0, start : start + TILE]


def energy_of(total, span):
    return pl.pallas_call(
        functools.partial(energy_kernel, span),
        out_shape=jax.ShapeDtypeStruct((total.shape[0] // span * 8, TILE), jnp.float32),
        in_specs=[VMEM],
        out_specs=VMEM,
        compiler_params=params(8),
        name="energy",
    )(total)


def combine_kernel(first, groups, mine_ref, moved_ref, energy_ref, energy_moved_ref, *out_refs):
    count = len(out_refs)
    span = mine_ref.shape[0] // count
    for i in range(count):
        rows = slice(i * span, (i + 1) * span)
        theirs = slice((first + i) * 8, (first + i + 1) * 8)
        mine = slice((groups + first + i) * 8, (groups + first + i + 1) * 8)
        out_refs[i][:span, :] = mine_ref[rows, :] + moved_ref[rows, :]
        out_refs[i][span:, :] = energy_ref[mine, :] + energy_moved_ref[theirs, :]


def combine(first, count, groups, mine, moved, energy, energy_moved):
    shape = (mine.shape[0] // count + 8, mine.shape[1])
    return pl.pallas_call(
        functools.partial(combine_kernel, first, groups),
        out_shape=[jax.ShapeDtypeStruct(shape, jnp.float32)] * count,
        in_specs=[VMEM] * 4,
        out_specs=[VMEM] * count,
        compiler_params=params(4),
        name="combine",
    )(mine, moved, energy, energy_moved)


def finish_kernel(nodes, count, *refs):
    parts, (source_ref, current_ref, inverse_ref) = refs[:count], refs[count:]
    span = source_ref.shape[0]
    energy = parts[0][span:, :]
    product = parts[0][:span, :]
    for part in parts[1:]:
        energy += part[span:, :]
        product += part[:span, :]
    row = lax.broadcasted_iota(jnp.int32, (8, TILE), 0)
    for half in range(span // TILE):
        rows = slice(half * TILE, (half + 1) * TILE)
        column = lax.dot_general(
            energy,
            (row == half).astype(jnp.float32),
            (((0,), (0,)), ((), ())),
            precision=lax.Precision.HIGHEST,
            preferred_element_type=jnp.float32,
        )
        norm = jnp.sqrt(jnp.float32(nodes)) * jnp.sqrt(column / nodes + EPSILON)
        inverse = 1.0 / norm
        inverse_ref[rows, :] = inverse
        current_ref[rows, :] = jnp.tanh(
            RETAIN * (product[rows, :] * inverse) + TELEPORT * source_ref[rows, :]
        )


def finish(nodes, parts, source):
    shape = jax.ShapeDtypeStruct(source.shape, jnp.float32)
    return pl.pallas_call(
        functools.partial(finish_kernel, nodes, len(parts)),
        out_shape=[shape, shape],
        in_specs=[VMEM] * (len(parts) + 1),
        out_specs=[VMEM, VMEM],
        compiler_params=params(4),
        name="finish",
    )(*parts, source)


def fence_kernel(out_ref):
    out_ref[...] = jnp.zeros_like(out_ref)


def fence():
    return pl.pallas_call(
        fence_kernel,
        out_shape=jax.ShapeDtypeStruct((8, TILE), jnp.float32),
        out_specs=VMEM,
        compiler_params=params(1),
        cost_estimate=pl.CostEstimate(flops=10**10, bytes_accessed=10**8, transcendentals=0),
        name="fence",
    )()


def multiply_kernel(first_row, first, count, add, adjacency_ref, *refs):
    features, refs = refs[:count], refs[count:]
    total_ref = refs[0] if add else None
    out_ref, both_ref = refs[-2:]
    span, width = features[0].shape
    for i in range(count):
        x = features[i][...]
        high = x.astype(jnp.bfloat16)
        rows = slice(i * span, (i + 1) * span)
        both_ref[rows, :width] = high
        both_ref[rows, width:] = (x - high.astype(jnp.float32)).astype(jnp.bfloat16)
    tile = min(out_ref.shape[0], 2048)
    for start in range(0, out_ref.shape[0], tile):
        rows = slice(first_row + start, first_row + start + tile)
        both = jnp.dot(
            adjacency_ref[rows, first * span : (first + count) * span],
            both_ref[...],
            preferred_element_type=jnp.float32,
        )
        sums = both[:, :width] + both[:, width:]
        if add:
            sums += total_ref[rows, :]
        out_ref[start : start + tile, :] = sums


def multiply(adjacency, first_row, row_count, first, features, total=None):
    span, width = features[0].shape
    count = len(features)
    add = total is not None
    return pl.pallas_call(
        functools.partial(multiply_kernel, first_row, first, count, add),
        out_shape=jax.ShapeDtypeStruct((row_count, width), jnp.float32),
        in_specs=[VMEM] * (1 + count + add),
        out_specs=VMEM,
        scratch_shapes=[pltpu.VMEM((count * span, 2 * width), jnp.bfloat16)],
        compiler_params=params(8),
        cost_estimate=pl.CostEstimate(
            flops=4 * row_count * count * span * width,
            bytes_accessed=2 * row_count * count * span,
            transcendentals=0,
        ),
        name="multiply",
    )(adjacency, *features, *([total] if add else []))


def far_offsets(groups):
    return [groups - 1] + list(range(1, groups - 1)) + [0] if groups > 1 else [0]


def shards(source, value, occupancy, exponent):
    row_size, col_size = lax.axis_size("row"), lax.axis_size("col")
    span = source.shape[0]
    nodes = value.shape[0] * row_size
    groups = col_size // 2
    half = groups * span
    offsets = far_offsets(groups)
    cuts = [(0, 1), (1, groups - 1)] if groups > 1 else [(0, 1)]

    started = fence()
    current = source
    for step in range(STEPS):
        features = [current]
        for d in range(1, row_size):
            features.append(swap(current, "row", row_size, d))
        if step == 0:
            adjacency, squares = prepare(
                value, occupancy, exponent, started, offsets, span
            )
            energy = energy_of(squares, span)
            energy_moved = swap(energy[: 8 * groups], "col", col_size, 1)
        first = multiply(adjacency, 0, 2 * half, 0, features[:1])
        if row_size > 2:
            first = multiply(adjacency, 0, 2 * half, 1, features[1:-1], first)
        last = features[-1:]
        moved = []
        for start, count in cuts:
            other = multiply(adjacency, start * span, count * span, row_size - 1, last, first)
            moved.append(swap(other, "col", col_size, 1))
        sums = []
        for i, (start, count) in enumerate(cuts):
            mine = multiply(adjacency, half + start * span, count * span, row_size - 1, last, first)
            if step == 0:
                sums += combine(start, count, groups, mine, moved[i], energy, energy_moved)
            else:
                for d in range(count):
                    rows = slice(d * span, (d + 1) * span)
                    sums.append(mine[rows] + moved[i][rows])
        parts = [
            swap(part, "col", col_size, 2 * offset) if offset else part
            for offset, part in zip(offsets, sums)
        ]
        if step == 0:
            current, inverse = finish(nodes, parts, source)
        else:
            product = functools.reduce(jnp.add, parts)
            current = jnp.tanh(RETAIN * (product * inverse) + TELEPORT * source)
    return current


def solution(mesh):
    placed = (P(("row", "col"), None), P("row", "col"), P("row", "col"), P("row", "col"))
    return jax.shard_map(
        shards, mesh=mesh, in_specs=placed, out_specs=P(("row", "col"), None), check_vma=False
    )
```

```python
import functools

import jax
import jax.numpy as jnp
from jax import lax
from jax.experimental import pallas as pl
from jax.experimental.pallas import tpu as pltpu
from jax.sharding import PartitionSpec as P


STEPS = 3
TILE = 128
EPSILON = 1e-05
RETAIN = 0.8
TELEPORT = 0.2
VMEM = pl.BlockSpec(memory_space=pltpu.VMEM)


def params(mib):
    return pltpu.CompilerParams(vmem_limit_bytes=mib * 1024 * 1024)


def swap(array, axis, size, offset):
    return lax.ppermute(array, axis, [(i, i ^ offset) for i in range(size)])


def prepare_kernel(offsets, near, fence_ref, present_ref, power_ref, value_ref, out_ref, energy_ref, held, scales, arrived):
    blocks, span, _ = held.shape
    parts, chunks = span // TILE, len(near)
    row, col = lax.axis_index("row"), lax.axis_index("col")
    sources = [col ^ (2 * offset + 1 - side) for side in range(2) for offset in offsets]

    def copy(i, chunk):
        rows = pl.ds(pl.multiple_of(sources[i] * span, span), span)
        cols = pl.ds(pl.multiple_of((row ^ near[chunk]) * span, span), span)
        target = held.at[i, :, pl.ds(chunk * span, span)]
        return pltpu.make_async_copy(value_ref.at[rows, cols], target, arrived.at[i, chunk])

    for i in range(blocks):
        for chunk in range(chunks):
            copy(i, chunk).start()
    table = (present_ref[...] << (power_ref[...] + 3)).astype(jnp.float32) * 0.125
    shape = (table.shape[0], scales.shape[1])
    owner = lax.broadcasted_iota(jnp.int32, shape, 1) // TILE
    spread = owner == lax.broadcasted_iota(jnp.int32, shape, 0)
    scales[...] = lax.dot_general(
        table.astype(jnp.bfloat16),
        spread.astype(jnp.bfloat16),
        (((0,), (0,)), ((), ())),
        preferred_element_type=jnp.float32,
    )
    for i in range(blocks):
        for chunk in range(chunks):
            copy(i, chunk).wait()
        for half in range(parts):
            from_rows = slice(half * TILE, (half + 1) * TILE)
            to_rows = slice(i * span + half * TILE, i * span + (half + 1) * TILE)
            row_tile = pl.ds(sources[i] * parts + half, 1)
            total = jnp.zeros((TILE, TILE), jnp.float32)
            for chunk in range(chunks):
                cols = slice(chunk * span, (chunk + 1) * span)
                from_cols = pl.ds(pl.multiple_of((row ^ near[chunk]) * span, span), span)
                scaled = held[i, from_rows, cols].astype(jnp.float32) * scales[row_tile, from_cols]
                out_ref[to_rows, cols] = scaled.astype(jnp.bfloat16)
                squares = scaled * scaled
                for part in range(parts):
                    total += squares[:, part * TILE : (part + 1) * TILE]
            energy_ref[to_rows, :] = total


def prepare(value, present, power, fence, offsets, near, span):
    row_count, col_count = value.shape
    blocks, chunks = row_count // span, col_count // span
    return pl.pallas_call(
        functools.partial(prepare_kernel, offsets, near),
        in_specs=[VMEM] * 3 + [pl.BlockSpec(memory_space=pltpu.HBM)],
        out_specs=[VMEM, VMEM],
        out_shape=[
            jax.ShapeDtypeStruct(value.shape, jnp.bfloat16),
            jax.ShapeDtypeStruct((row_count, TILE), jnp.float32),
        ],
        scratch_shapes=[
            pltpu.VMEM((blocks, span, col_count), jnp.bfloat16),
            pltpu.VMEM((row_count // TILE, col_count), jnp.float32),
            pltpu.SemaphoreType.DMA((blocks, chunks)),
        ],
        compiler_params=params(48),
        name="prepare",
    )(fence, present.T, power.T, value)


def energy_kernel(span, total_ref, out_ref):
    total = total_ref[...]
    ones = jnp.ones((8, TILE), jnp.bfloat16)
    sums = jnp.zeros((8, total.shape[0]), jnp.float32)
    for _ in range(3):
        piece = total.astype(jnp.bfloat16)
        total -= piece.astype(jnp.float32)
        sums += lax.dot_general(
            ones, piece, (((1,), (1,)), ((), ())), preferred_element_type=jnp.float32
        )
    out_ref[...] = jnp.zeros_like(out_ref)
    for block in range(sums.shape[1] // span):
        for part in range(span // TILE):
            start = block * span + part * TILE
            out_ref[block * 8 + part, :] = sums[0, start : start + TILE]


def energy_of(total, span):
    return pl.pallas_call(
        functools.partial(energy_kernel, span),
        out_shape=jax.ShapeDtypeStruct((total.shape[0] // span * 8, TILE), jnp.float32),
        in_specs=[VMEM],
        out_specs=VMEM,
        compiler_params=params(8),
        name="energy",
    )(total)


def combine_kernel(first, groups, mine_ref, moved_ref, energy_ref, energy_moved_ref, *out_refs):
    count = len(out_refs)
    span = mine_ref.shape[0] // count
    for i in range(count):
        rows = slice(i * span, (i + 1) * span)
        theirs = slice((first + i) * 8, (first + i + 1) * 8)
        mine = slice((groups + first + i) * 8, (groups + first + i + 1) * 8)
        out_refs[i][:span, :] = mine_ref[rows, :] + moved_ref[rows, :]
        out_refs[i][span:, :] = energy_ref[mine, :] + energy_moved_ref[theirs, :]


def combine(first, count, groups, mine, moved, energy, energy_moved):
    shape = (mine.shape[0] // count + 8, mine.shape[1])
    return pl.pallas_call(
        functools.partial(combine_kernel, first, groups),
        out_shape=[jax.ShapeDtypeStruct(shape, jnp.float32)] * count,
        in_specs=[VMEM] * 4,
        out_specs=[VMEM] * count,
        compiler_params=params(4),
        name="combine",
    )(mine, moved, energy, energy_moved)


def finish_kernel(nodes, count, *refs):
    parts, (source_ref, current_ref, inverse_ref) = refs[:count], refs[count:]
    span = source_ref.shape[0]
    energy = parts[0][span:, :]
    product = parts[0][:span, :]
    for part in parts[1:]:
        energy += part[span:, :]
        product += part[:span, :]
    row = lax.broadcasted_iota(jnp.int32, (8, TILE), 0)
    for half in range(span // TILE):
        rows = slice(half * TILE, (half + 1) * TILE)
        column = lax.dot_general(
            energy,
            (row == half).astype(jnp.float32),
            (((0,), (0,)), ((), ())),
            precision=lax.Precision.HIGHEST,
            preferred_element_type=jnp.float32,
        )
        norm = jnp.sqrt(jnp.float32(nodes)) * jnp.sqrt(column / nodes + EPSILON)
        inverse = 1.0 / norm
        inverse_ref[rows, :] = inverse
        current_ref[rows, :] = jnp.tanh(
            RETAIN * (product[rows, :] * inverse) + TELEPORT * source_ref[rows, :]
        )


def finish(nodes, parts, source):
    shape = jax.ShapeDtypeStruct(source.shape, jnp.float32)
    return pl.pallas_call(
        functools.partial(finish_kernel, nodes, len(parts)),
        out_shape=[shape, shape],
        in_specs=[VMEM] * (len(parts) + 1),
        out_specs=[VMEM, VMEM],
        compiler_params=params(4),
        name="finish",
    )(*parts, source)


def fence_kernel(out_ref):
    out_ref[...] = jnp.zeros_like(out_ref)


def fence():
    return pl.pallas_call(
        fence_kernel,
        out_shape=jax.ShapeDtypeStruct((8, TILE), jnp.float32),
        out_specs=VMEM,
        compiler_params=params(1),
        cost_estimate=pl.CostEstimate(flops=10**10, bytes_accessed=10**8, transcendentals=0),
        name="fence",
    )()


def multiply_kernel(first_row, first, count, add, adjacency_ref, *refs):
    features, refs = refs[:count], refs[count:]
    total_ref = refs[0] if add else None
    out_ref, both_ref = refs[-2:]
    span, width = features[0].shape
    for i in range(count):
        x = features[i][...]
        high = x.astype(jnp.bfloat16)
        rows = slice(i * span, (i + 1) * span)
        both_ref[rows, :width] = high
        both_ref[rows, width:] = (x - high.astype(jnp.float32)).astype(jnp.bfloat16)
    tile = min(out_ref.shape[0], 2048)
    for start in range(0, out_ref.shape[0], tile):
        rows = slice(first_row + start, first_row + start + tile)
        both = jnp.dot(
            adjacency_ref[rows, first * span : (first + count) * span],
            both_ref[...],
            preferred_element_type=jnp.float32,
        )
        sums = both[:, :width] + both[:, width:]
        if add:
            sums += total_ref[rows, :]
        out_ref[start : start + tile, :] = sums


def multiply(adjacency, first_row, row_count, first, features, total=None):
    span, width = features[0].shape
    count = len(features)
    add = total is not None
    return pl.pallas_call(
        functools.partial(multiply_kernel, first_row, first, count, add),
        out_shape=jax.ShapeDtypeStruct((row_count, width), jnp.float32),
        in_specs=[VMEM] * (1 + count + add),
        out_specs=VMEM,
        scratch_shapes=[pltpu.VMEM((count * span, 2 * width), jnp.bfloat16)],
        compiler_params=params(8),
        cost_estimate=pl.CostEstimate(
            flops=4 * row_count * count * span * width,
            bytes_accessed=2 * row_count * count * span,
            transcendentals=0,
        ),
        name="multiply",
    )(adjacency, *features, *([total] if add else []))


def near_offsets(size):
    return [size - 1] + list(range(1, size - 1))


def far_offsets(groups):
    return [groups - 1] + list(range(1, groups - 1)) + [0] if groups > 1 else [0]


def shards(source, value, occupancy, exponent):
    row_size, col_size = lax.axis_size("row"), lax.axis_size("col")
    span = source.shape[0]
    nodes = value.shape[0] * row_size
    groups = col_size // 2
    half = groups * span
    offsets, near = far_offsets(groups), near_offsets(row_size)
    cuts = [(0, 1), (1, groups - 1)] if groups > 1 else [(0, 1)]

    started = fence()
    current = source
    for step in range(STEPS):
        features = [current]
        for d in near:
            features.append(swap(current, "row", row_size, d))
        if step == 0:
            adjacency, squares = prepare(
                value, occupancy, exponent, started, offsets, [0] + near, span
            )
            energy = energy_of(squares, span)
            energy_moved = swap(energy[: 8 * groups], "col", col_size, 1)
        first = multiply(adjacency, 0, 2 * half, 0, features[:1])
        if row_size > 2:
            first = multiply(adjacency, 0, 2 * half, 1, features[1:-1], first)
        last = features[-1:]
        moved = []
        for start, count in cuts:
            other = multiply(adjacency, start * span, count * span, row_size - 1, last, first)
            moved.append(swap(other, "col", col_size, 1))
        sums = []
        for i, (start, count) in enumerate(cuts):
            mine = multiply(adjacency, half + start * span, count * span, row_size - 1, last, first)
            if step == 0:
                sums += combine(start, count, groups, mine, moved[i], energy, energy_moved)
            else:
                for d in range(count):
                    rows = slice(d * span, (d + 1) * span)
                    sums.append(mine[rows] + moved[i][rows])
        parts = [
            swap(part, "col", col_size, 2 * offset) if offset else part
            for offset, part in zip(offsets, sums)
        ]
        if step == 0:
            current, inverse = finish(nodes, parts, source)
        else:
            product = functools.reduce(jnp.add, parts)
            current = jnp.tanh(RETAIN * (product * inverse) + TELEPORT * source)
    return current


def solution(mesh):
    placed = (P(("row", "col"), None), P("row", "col"), P("row", "col"), P("row", "col"))
    return jax.shard_map(
        shards, mesh=mesh, in_specs=placed, out_specs=P(("row", "col"), None), check_vma=False
    )
```

```python
import functools

import jax
import jax.numpy as jnp
from jax import lax
from jax.experimental import pallas as pl
from jax.experimental.pallas import tpu as pltpu
from jax.sharding import PartitionSpec as P


STEPS = 3
STAGGER = 35
TILE = 128
EPSILON = 1e-05
RETAIN = 0.8
TELEPORT = 0.2
VMEM = pl.BlockSpec(memory_space=pltpu.VMEM)


def params(mib):
    return pltpu.CompilerParams(vmem_limit_bytes=mib * 1024 * 1024)


def swap(array, axis, size, offset):
    return lax.ppermute(array, axis, [(i, i ^ offset) for i in range(size)])


def swap_far(array, size, offsets):
    return lax.ppermute(array, "col", [(i, i ^ (2 * offsets[i % 2])) for i in range(size)])


def prepare_kernel(offsets, near, fence_ref, present_ref, power_ref, value_ref, out_ref, energy_ref, held, scales, arrived):
    blocks, span, _ = held.shape
    parts, chunks = span // TILE, len(near)
    row, col = lax.axis_index("row"), lax.axis_index("col")
    odd = lax.rem(col, 2)
    sources = []
    for side in range(2):
        core = odd if side else 1 - odd
        for even_offset, odd_offset in offsets:
            offset = even_offset + core * (odd_offset - even_offset)
            sources.append(col ^ (2 * offset + 1 - side))

    def copy(i, chunk):
        rows = pl.ds(pl.multiple_of(sources[i] * span, span), span)
        cols = pl.ds(pl.multiple_of((row ^ near[chunk]) * span, span), span)
        target = held.at[i, :, pl.ds(chunk * span, span)]
        return pltpu.make_async_copy(value_ref.at[rows, cols], target, arrived.at[i, chunk])

    for i in range(blocks):
        for chunk in range(chunks):
            copy(i, chunk).start()
    table = (present_ref[...] << (power_ref[...] + 3)).astype(jnp.float32) * 0.125
    shape = (table.shape[0], scales.shape[1])
    owner = lax.broadcasted_iota(jnp.int32, shape, 1) // TILE
    spread = owner == lax.broadcasted_iota(jnp.int32, shape, 0)
    scales[...] = lax.dot_general(
        table.astype(jnp.bfloat16),
        spread.astype(jnp.bfloat16),
        (((0,), (0,)), ((), ())),
        preferred_element_type=jnp.float32,
    )
    for i in range(blocks):
        for chunk in range(chunks):
            copy(i, chunk).wait()
        for half in range(parts):
            from_rows = slice(half * TILE, (half + 1) * TILE)
            to_rows = slice(i * span + half * TILE, i * span + (half + 1) * TILE)
            row_tile = pl.ds(sources[i] * parts + half, 1)
            total = jnp.zeros((TILE, TILE), jnp.float32)
            for chunk in range(chunks):
                cols = slice(chunk * span, (chunk + 1) * span)
                from_cols = pl.ds(pl.multiple_of((row ^ near[chunk]) * span, span), span)
                scaled = held[i, from_rows, cols].astype(jnp.float32) * scales[row_tile, from_cols]
                out_ref[to_rows, cols] = scaled.astype(jnp.bfloat16)
                squares = scaled * scaled
                for part in range(parts):
                    total += squares[:, part * TILE : (part + 1) * TILE]
            energy_ref[to_rows, :] = total


def prepare(value, present, power, fence, offsets, near, span):
    row_count, col_count = value.shape
    blocks, chunks = row_count // span, col_count // span
    return pl.pallas_call(
        functools.partial(prepare_kernel, offsets, near),
        in_specs=[VMEM] * 3 + [pl.BlockSpec(memory_space=pltpu.HBM)],
        out_specs=[VMEM, VMEM],
        out_shape=[
            jax.ShapeDtypeStruct(value.shape, jnp.bfloat16),
            jax.ShapeDtypeStruct((row_count, TILE), jnp.float32),
        ],
        scratch_shapes=[
            pltpu.VMEM((blocks, span, col_count), jnp.bfloat16),
            pltpu.VMEM((row_count // TILE, col_count), jnp.float32),
            pltpu.SemaphoreType.DMA((blocks, chunks)),
        ],
        compiler_params=params(48),
        name="prepare",
    )(fence, present.T, power.T, value)


def energy_kernel(span, total_ref, out_ref):
    total = total_ref[...]
    ones = jnp.ones((8, TILE), jnp.bfloat16)
    sums = jnp.zeros((8, total.shape[0]), jnp.float32)
    for _ in range(3):
        piece = total.astype(jnp.bfloat16)
        total -= piece.astype(jnp.float32)
        sums += lax.dot_general(
            ones, piece, (((1,), (1,)), ((), ())), preferred_element_type=jnp.float32
        )
    out_ref[...] = jnp.zeros_like(out_ref)
    for block in range(sums.shape[1] // span):
        for part in range(span // TILE):
            start = block * span + part * TILE
            out_ref[block * 8 + part, :] = sums[0, start : start + TILE]


def energy_of(total, span):
    return pl.pallas_call(
        functools.partial(energy_kernel, span),
        out_shape=jax.ShapeDtypeStruct((total.shape[0] // span * 8, TILE), jnp.float32),
        in_specs=[VMEM],
        out_specs=VMEM,
        compiler_params=params(8),
        name="energy",
    )(total)


def combine_kernel(first, groups, mine_ref, moved_ref, energy_ref, energy_moved_ref, *out_refs):
    count = len(out_refs)
    span = mine_ref.shape[0] // count
    for i in range(count):
        rows = slice(i * span, (i + 1) * span)
        theirs = slice((first + i) * 8, (first + i + 1) * 8)
        mine = slice((groups + first + i) * 8, (groups + first + i + 1) * 8)
        out_refs[i][:span, :] = mine_ref[rows, :] + moved_ref[rows, :]
        out_refs[i][span:, :] = energy_ref[mine, :] + energy_moved_ref[theirs, :]


def combine(first, count, groups, mine, moved, energy, energy_moved):
    shape = (mine.shape[0] // count + 8, mine.shape[1])
    return pl.pallas_call(
        functools.partial(combine_kernel, first, groups),
        out_shape=[jax.ShapeDtypeStruct(shape, jnp.float32)] * count,
        in_specs=[VMEM] * 4,
        out_specs=[VMEM] * count,
        compiler_params=params(4),
        name="combine",
    )(mine, moved, energy, energy_moved)


def finish_kernel(nodes, count, *refs):
    parts, (source_ref, current_ref, inverse_ref) = refs[:count], refs[count:]
    span = source_ref.shape[0]
    energy = parts[0][span:, :]
    product = parts[0][:span, :]
    for part in parts[1:]:
        energy += part[span:, :]
        product += part[:span, :]
    row = lax.broadcasted_iota(jnp.int32, (8, TILE), 0)
    for half in range(span // TILE):
        rows = slice(half * TILE, (half + 1) * TILE)
        column = lax.dot_general(
            energy,
            (row == half).astype(jnp.float32),
            (((0,), (0,)), ((), ())),
            precision=lax.Precision.HIGHEST,
            preferred_element_type=jnp.float32,
        )
        norm = jnp.sqrt(jnp.float32(nodes)) * jnp.sqrt(column / nodes + EPSILON)
        inverse = 1.0 / norm
        inverse_ref[rows, :] = inverse
        current_ref[rows, :] = jnp.tanh(
            RETAIN * (product[rows, :] * inverse) + TELEPORT * source_ref[rows, :]
        )


def finish(nodes, parts, source):
    shape = jax.ShapeDtypeStruct(source.shape, jnp.float32)
    return pl.pallas_call(
        functools.partial(finish_kernel, nodes, len(parts)),
        out_shape=[shape, shape],
        in_specs=[VMEM] * (len(parts) + 1),
        out_specs=[VMEM, VMEM],
        compiler_params=params(4),
        name="finish",
    )(*parts, source)


def fence_kernel(out_ref):
    out_ref[...] = jnp.zeros_like(out_ref)


def fence():
    return pl.pallas_call(
        fence_kernel,
        out_shape=jax.ShapeDtypeStruct((8, TILE), jnp.float32),
        out_specs=VMEM,
        compiler_params=params(1),
        cost_estimate=pl.CostEstimate(flops=10**10, bytes_accessed=10**8, transcendentals=0),
        name="fence",
    )()


def multiply_kernel(first_row, first, count, add, adjacency_ref, *refs):
    features, refs = refs[:count], refs[count:]
    total_ref = refs[0] if add else None
    out_ref, both_ref = refs[-2:]
    span, width = features[0].shape
    for i in range(count):
        x = features[i][...]
        high = x.astype(jnp.bfloat16)
        rows = slice(i * span, (i + 1) * span)
        both_ref[rows, :width] = high
        both_ref[rows, width:] = (x - high.astype(jnp.float32)).astype(jnp.bfloat16)
    tile = min(out_ref.shape[0], 2048)
    for start in range(0, out_ref.shape[0], tile):
        rows = slice(first_row + start, first_row + start + tile)
        both = jnp.dot(
            adjacency_ref[rows, first * span : (first + count) * span],
            both_ref[...],
            preferred_element_type=jnp.float32,
        )
        sums = both[:, :width] + both[:, width:]
        if add:
            sums += total_ref[rows, :]
        out_ref[start : start + tile, :] = sums


def multiply(adjacency, first_row, row_count, first, features, total=None):
    span, width = features[0].shape
    count = len(features)
    add = total is not None
    return pl.pallas_call(
        functools.partial(multiply_kernel, first_row, first, count, add),
        out_shape=jax.ShapeDtypeStruct((row_count, width), jnp.float32),
        in_specs=[VMEM] * (1 + count + add),
        out_specs=VMEM,
        scratch_shapes=[pltpu.VMEM((count * span, 2 * width), jnp.bfloat16)],
        compiler_params=params(8),
        cost_estimate=pl.CostEstimate(
            flops=4 * row_count * count * span * width,
            bytes_accessed=2 * row_count * count * span,
            transcendentals=0,
        ),
        name="multiply",
    )(adjacency, *features, *([total] if add else []))


def near_offsets(size):
    return list(range(size - 2, 0, -1)) + [size - 1]


def far_offsets(groups):
    even = list(range(groups - 1, -1, -1))
    odd = [groups - 1] + list(range(1, groups - 1)) + [0]
    return list(zip(even, odd))


def stagger_kernel(in_ref, out_ref, done):
    count = 1 + lax.rem(lax.axis_index("col"), 2) * STAGGER

    def body(i, carry):
        copy = pltpu.make_async_copy(in_ref, out_ref, done)
        copy.start()
        copy.wait()
        return carry

    lax.fori_loop(0, count, body, 0)


def stagger(array):
    return pl.pallas_call(
        stagger_kernel,
        out_shape=jax.ShapeDtypeStruct(array.shape, array.dtype),
        in_specs=[VMEM],
        out_specs=VMEM,
        scratch_shapes=[pltpu.SemaphoreType.DMA],
        compiler_params=params(4),
        name="stagger",
    )(array)


def shards(source, value, occupancy, exponent):
    row_size, col_size = lax.axis_size("row"), lax.axis_size("col")
    span = source.shape[0]
    nodes = value.shape[0] * row_size
    groups = col_size // 2
    half = groups * span
    offsets, near = far_offsets(groups), near_offsets(row_size)
    cuts = [(0, 1), (1, groups - 1)] if groups > 1 else [(0, 1)]

    started = fence()
    current = source
    for step in range(STEPS):
        features = [current]
        for d in near:
            features.append(swap(current, "row", row_size, d))
        if step == 0:
            adjacency, squares = prepare(
                value, occupancy, exponent, started, offsets, [0] + near, span
            )
            energy = energy_of(squares, span)
            energy_moved = swap(energy[: 8 * groups], "col", col_size, 1)
        first = multiply(adjacency, 0, 2 * half, 0, features[:1])
        if row_size > 2:
            first = multiply(adjacency, 0, 2 * half, 1, features[1:-1], first)
        last = features[-1:]
        moved = []
        for start, count in cuts:
            other = multiply(adjacency, start * span, count * span, row_size - 1, last, first)
            moved.append(swap(other, "col", col_size, 1))
        sums = []
        for i, (start, count) in enumerate(cuts):
            mine = multiply(adjacency, half + start * span, count * span, row_size - 1, last, first)
            if step == 0:
                sums += combine(start, count, groups, mine, moved[i], energy, energy_moved)
            else:
                for d in range(count):
                    rows = slice(d * span, (d + 1) * span)
                    sums.append(mine[rows] + moved[i][rows])
        if step < STEPS - 1:
            sums[0] = stagger(sums[0])
        parts = sums[-1:]
        for i in range(groups - 1):
            parts.append(swap_far(sums[i], col_size, offsets[i]))
        if step == 0:
            current, inverse = finish(nodes, parts, source)
        else:
            product = functools.reduce(jnp.add, parts)
            current = jnp.tanh(RETAIN * (product * inverse) + TELEPORT * source)
    return current


def solution(mesh):
    placed = (P(("row", "col"), None), P("row", "col"), P("row", "col"), P("row", "col"))
    return jax.shard_map(
        shards, mesh=mesh, in_specs=placed, out_specs=P(("row", "col"), None), check_vma=False
    )
```
